32 devices in a mesh: blk: 16 (over z, y, core), rep: 2 (over x).
Axes of the slice: x: 2, y: 2, z: 4, core: 2. Of those that a mesh axis runs over, the one named last changes fastest.
Arguments:
- raw_integrals: float32 [16, 1024, 512], P(None, 'blk'), may hold values from -0.6 to 0.6
- virtual_coeffs: float32 [512, 256], P(None, 'rep'), may hold values from -0.25 to 0.25
- metric_root: float32 [1024, 1024], P(None, 'rep'), may hold values from -1 to 3, as said below
- occ_energies: float32 [16], P('blk'), may hold values from -2 to -0.5
- virt_energies: float32 [256], replicated, may hold values from 0.2 to 3
Outputs:
- gamma: float32 [16, 256, 1024], P('blk', None, 'rep')
The draws below stay inside these ranges and needn't reach their ends.
Inputs may be any that keep to these rules, and one draw needn't show every extreme that they name: metric_root is exactly symmetric.
All inputs are finite; a program needn't handle non-finite values.
Results may differ from the reference program's by a relative error of at most 0.0001.
Values sent between devices are 32-bit elements; how exact they have to be, the bound alone decides.
No kernel may reach another device: no remote copies, remote signals or barrier semaphores. Data moves between devices by JAX's collectives and lax.ppermute only.
A program may use at most 64 MiB of HBM per device.

```python
import math
import jax
import jax.numpy as jnp
from jax import lax

OCC_DEV = 1
V = 256
NAUX = 1024
NAO = 512
OCC = 16
PAIR_BLOCKS = 4


def draw_metric_root(key, part):
    first_key = jax.random.fold_in(key, 11)
    second_key = jax.random.fold_in(key, 23)
    normal_part = jnp.clip(jax.random.normal(first_key, (NAUX, NAUX), jnp.float32), -4.0, 4.0)
    diagonal = jax.random.uniform(second_key, (NAUX,), jnp.float32, 1.0, 2.0)
    symmetric = 0.3 * (normal_part + normal_part.T) / math.sqrt(NAUX)
    return symmetric + jnp.diag(diagonal)


def block_levels(own_key, extent, shards, low, largest):
    def one(axis_at, blocks):
        heights = jax.random.uniform(jax.random.fold_in(jax.random.fold_in(own_key, 6), axis_at), (blocks,), jnp.float32, low / len(shards), largest / len(shards))
        return jnp.repeat(jnp.exp(heights), extent[axis_at] // blocks).reshape((-1,) + (1,) * (len(extent) - axis_at - 1))

    level = one(*shards[0])
    for cut in shards[1:]:
        level = level * one(*cut)
    return level


def noise(rng, dims, scale, most, cuts=(), dtype=jnp.bfloat16):
    entries = scale * jax.random.normal(rng, dims, jnp.float32)
    if cuts:
        entries = entries * block_levels(rng, dims, cuts, -0.22, 0.18)
    return jnp.clip(entries, -most, most).astype(dtype)


def setup_inputs(seed: int = 0) -> dict:
    arg_keys = jax.random.split(jax.random.key(seed), 6)
    raw_integrals = noise(arg_keys[0], (OCC, NAUX, NAO), 0.1, 0.6, ((1, 16),), jnp.float32)
    virtual_coeffs = noise(arg_keys[1], (NAO, V), NAO ** -0.5, 0.25, ((1, 2),), jnp.float32)
    metric_root = draw_metric_root(jax.random.fold_in(arg_keys[5], 71), 0)
    occ_energies = jnp.clip(-2.0 + 1.5 * jax.random.uniform(arg_keys[3], (OCC,), jnp.float32) ** block_levels(arg_keys[3], (OCC,), ((0, 16),), -0.2, 0.2), -2.0, -0.5)
    virt_energies = jnp.clip(jax.random.uniform(arg_keys[4], (V,), jnp.float32, 0.2, 3.0), 0.2, 3.0)
    return {"raw_integrals": raw_integrals, "virtual_coeffs": virtual_coeffs, "metric_root": metric_root, "occ_energies": occ_energies, "virt_energies": virt_energies}


def reference(raw_integrals, virtual_coeffs, metric_root, occ_energies, virt_energies):
    highest = lax.Precision.HIGHEST
    halfway = jnp.einsum("ipm,ma->ipa", raw_integrals, virtual_coeffs, precision=highest)
    fitted = jnp.einsum("ipa,pq->iaq", halfway, metric_root, precision=highest)
    spread = virt_energies[:, None] + virt_energies[None, :]
    block_count = OCC // OCC_DEV
    blocks = fitted.reshape(block_count, OCC_DEV, V, NAUX)
    eps_blocks = occ_energies.reshape(block_count, OCC_DEV)
    gradient = jnp.zeros(blocks.shape, jnp.float32)
    for distance in range(PAIR_BLOCKS):
        other = jnp.roll(blocks, distance, axis=0)
        other_eps = jnp.roll(eps_blocks, distance, axis=0)
        coulomb = jnp.einsum("kxaq,kybq->kxyab", blocks, other, precision=highest)
        denominator = spread[None, None, None] - eps_blocks[:, :, None, None, None] - other_eps[:, None, :, None, None]
        amplitude = (2.0 * coulomb - jnp.swapaxes(coulomb, 3, 4)) / denominator
        gradient = gradient + jnp.einsum("kxyab,kybq->kxaq", amplitude, other, precision=highest)
    return gradient.reshape(OCC, V, NAUX)
```

```python
import jax
import jax.numpy as jnp
from jax import lax
from jax.sharding import PartitionSpec as P

TURNS = 2


def from_behind(x, axis, by):
    count = lax.axis_size(axis)
    return lax.ppermute(x, axis, [(i, (i + by) % count) for i in range(count)])


def pair_terms(own_rows, own_eps, other_rows, other_eps, virt_energies, gradient):
    highest = lax.Precision.HIGHEST
    coulomb = jnp.einsum("xaq,ybq->xyab", own_rows, other_rows, precision=highest)
    spread = virt_energies[:, None] + virt_energies[None, :]
    denominator = spread[None, None] - own_eps[:, None, None, None] - other_eps[None, :, None, None]
    amplitude = (2.0 * coulomb - jnp.swapaxes(coulomb, 2, 3)) / denominator
    return gradient + jnp.einsum("xyab,ybq->xaq", amplitude, other_rows, precision=highest)


def any_replicas(raw_integrals, virtual_coeffs, metric_root, occ_energies, virt_energies):
    highest = lax.Precision.HIGHEST
    halfway = jnp.einsum("ipm,ma->ipa", raw_integrals, virtual_coeffs, precision=highest)
    regrouped = lax.all_to_all(halfway, "blk", split_axis=0, concat_axis=1, tiled=True)
    complete = lax.all_gather(regrouped, "rep", axis=2, tiled=True)
    fitted_part = jnp.einsum("xpa,pq->xaq", complete, metric_root, precision=highest)
    fitted = lax.all_gather(fitted_part, "rep", axis=2, tiled=True)
    replica = lax.axis_index("rep")
    replicas = lax.axis_size("rep")
    travel_rows = fitted
    travel_eps = occ_energies
    for bit_index in range((replicas - 1).bit_length()):
        shifted_rows, shifted_eps = from_behind(
            (travel_rows, travel_eps), "blk", (1 << bit_index) * TURNS
        )
        chosen = replica >> bit_index & 1 == 1
        travel_rows = jnp.where(chosen, shifted_rows, travel_rows)
        travel_eps = jnp.where(chosen, shifted_eps, travel_eps)
    gradient = jnp.zeros(fitted.shape, jnp.float32)

    def advance(turn_index, state_now):
        other_rows, other_eps, total = state_now
        total = pair_terms(fitted, occ_energies, other_rows, other_eps, virt_energies, total)
        other_rows, other_eps = from_behind((other_rows, other_eps), "blk", 1)
        return (other_rows, other_eps, total)

    travel_rows, travel_eps, gradient = lax.fori_loop(
        0, TURNS - 1, advance, (travel_rows, travel_eps, gradient)
    )
    gradient = pair_terms(fitted, occ_energies, travel_rows, travel_eps, virt_energies, gradient)
    return lax.psum_scatter(gradient, "rep", scatter_dimension=2, tiled=True)


def dot(x, y, over_x, over_y):
    return lax.dot_general(
        x, y, (((over_x,), (over_y,)), ((), ())), precision=lax.Precision.HIGH
    )


def half_of(x, index, axis):
    size = x.shape[axis] // 2
    return lax.dynamic_slice_in_dim(x, index * size, size, axis)


def two_replicas(raw_integrals, virtual_coeffs, metric_root, occ_energies, virt_energies):
    blocks = lax.axis_size("blk")
    block = lax.axis_index("blk")
    rep = lax.axis_index("rep")
    core = block % 2
    swap = [(0, 1), (1, 0)]
    mate = [(i, i ^ 1) for i in range(blocks)]
    mine = half_of(metric_root, rep, 0)
    across = half_of(metric_root, 1 - rep, 0)
    there = lax.ppermute(half_of(mine, core, 0), "rep", swap)

    halfway = jnp.einsum(
        "ipm,ma->ipa", raw_integrals, virtual_coeffs, precision=lax.Precision.HIGH
    )
    note = jnp.broadcast_to(occ_energies[:, None, None], (halfway.shape[0], 8, halfway.shape[2]))
    sent = jnp.concatenate([halfway, note], axis=1)
    got = lax.all_to_all(sent, "blk", split_axis=0, concat_axis=0, tiled=True)
    depth = halfway.shape[1]
    rows = got[:, :depth].reshape(-1, got.shape[2])
    all_eps = got[:, depth, 0]

    there_mate = lax.ppermute(there, "blk", mate)
    fit_mine = dot(rows, metric_root, 0, 0)
    rows_there = half_of(rows, 1 - rep, 0)
    fit_there = (
        dot(half_of(rows, rep, 0), across, 0, 1)
        + dot(half_of(rows_there, core, 0), there, 0, 0)
        + dot(half_of(rows_there, 1 - core, 0), there_mate, 0, 0)
    )
    fit = jnp.where(
        rep == 0,
        jnp.concatenate([fit_mine, fit_there], 1),
        jnp.concatenate([fit_there, fit_mine], 1),
    )
    fit_over = lax.ppermute(fit, "rep", swap)
    behind = from_behind(fit, "blk", 2)
    own = jnp.concatenate([fit, fit_over], 0)
    behind_over = lax.ppermute(behind, "rep", swap)
    far = lax.ppermute(own, "blk", [(i, (i + 1 + 2 * (i % 2)) % blocks) for i in range(blocks)])
    near = jnp.concatenate([behind, behind_over], 0)
    near_mate = lax.ppermute(near, "blk", mate)

    eps = lambda index: lax.dynamic_index_in_dim(all_eps, index % blocks, 0, keepdims=False)
    levels = jnp.where(rep == 0, virt_energies, jnp.roll(virt_energies, virt_energies.shape[0] // 2))
    spread = levels[:, None] + levels[None, :] - eps(block)
    total = 0.0
    for other, index in (
        (own, block),
        (far, jnp.where(core == 0, block - 3, block - 1)),
        (near, block - 2),
        (near_mate, jnp.where(core == 0, block - 1, block - 3)),
    ):
        coulomb = dot(own, other, 1, 1)
        amplitude = (2.0 * coulomb - coulomb.T) / (spread - eps(index))
        total = total + dot(amplitude, half_of(other, rep, 1), 1, 0)
    total = jnp.where(rep == 0, total, jnp.roll(total, total.shape[0] // 2, 0))
    return total[None]


def per_device(*arrays):
    blocks = lax.axis_size("blk")
    if lax.axis_size("rep") == 2 and TURNS == 2 and blocks % 2 == 0 and arrays[3].shape == (1,):
        return two_replicas(*arrays)
    return any_replicas(*arrays)


def solution(mesh):
    return jax.shard_map(
        per_device,
        mesh=mesh,
        in_specs=(P(None, "blk", None), P(None, "rep"), P(None, "rep"), P("blk"), P()),
        out_specs=P("blk", None, "rep"),
        check_vma=False,
    )
```

```python
import math

import jax
import jax.numpy as jnp
from jax import lax
from jax.experimental import pallas as pl
from jax.experimental.pallas import tpu as pltpu
from jax.sharding import PartitionSpec as P

TURNS = 2
VMEM = 24 << 20


def from_behind(x, axis, by):
    count = lax.axis_size(axis)
    return lax.ppermute(x, axis, [(i, (i + by) % count) for i in range(count)])


def pair_terms(own_rows, own_eps, other_rows, other_eps, virt_energies, gradient):
    highest = lax.Precision.HIGHEST
    coulomb = jnp.einsum("xaq,ybq->xyab", own_rows, other_rows, precision=highest)
    spread = virt_energies[:, None] + virt_energies[None, :]
    denominator = spread[None, None] - own_eps[:, None, None, None] - other_eps[None, :, None, None]
    amplitude = (2.0 * coulomb - jnp.swapaxes(coulomb, 2, 3)) / denominator
    return gradient + jnp.einsum("xyab,ybq->xaq", amplitude, other_rows, precision=highest)


def any_replicas(raw_integrals, virtual_coeffs, metric_root, occ_energies, virt_energies):
    highest = lax.Precision.HIGHEST
    halfway = jnp.einsum("ipm,ma->ipa", raw_integrals, virtual_coeffs, precision=highest)
    regrouped = lax.all_to_all(halfway, "blk", split_axis=0, concat_axis=1, tiled=True)
    complete = lax.all_gather(regrouped, "rep", axis=2, tiled=True)
    fitted_part = jnp.einsum("xpa,pq->xaq", complete, metric_root, precision=highest)
    fitted = lax.all_gather(fitted_part, "rep", axis=2, tiled=True)
    replica = lax.axis_index("rep")
    replicas = lax.axis_size("rep")
    travel_rows = fitted
    travel_eps = occ_energies
    for bit_index in range((replicas - 1).bit_length()):
        shifted_rows, shifted_eps = from_behind(
            (travel_rows, travel_eps), "blk", (1 << bit_index) * TURNS
        )
        chosen = replica >> bit_index & 1 == 1
        travel_rows = jnp.where(chosen, shifted_rows, travel_rows)
        travel_eps = jnp.where(chosen, shifted_eps, travel_eps)
    gradient = jnp.zeros(fitted.shape, jnp.float32)

    def advance(turn_index, state_now):
        other_rows, other_eps, total = state_now
        total = pair_terms(fitted, occ_energies, other_rows, other_eps, virt_energies, total)
        other_rows, other_eps = from_behind((other_rows, other_eps), "blk", 1)
        return (other_rows, other_eps, total)

    travel_rows, travel_eps, gradient = lax.fori_loop(
        0, TURNS - 1, advance, (travel_rows, travel_eps, gradient)
    )
    gradient = pair_terms(fitted, occ_energies, travel_rows, travel_eps, virt_energies, gradient)
    return lax.psum_scatter(gradient, "rep", scatter_dimension=2, tiled=True)


def split(x):
    high = x.astype(jnp.bfloat16)
    return high, (x - high.astype(jnp.float32)).astype(jnp.bfloat16)


def product(x, y, over_x=1, over_y=0):
    one = lambda p, q: lax.dot_general(
        p, q, (((over_x,), (over_y,)), ((), ())), preferred_element_type=jnp.float32
    )
    return one(x[0], y[0]) + (one(x[0], y[1]) + one(x[1], y[0]))


def transform_kernel(raw_ref, coeffs_ref, eps_ref, out_ref, high_ref, low_ref):
    depth = raw_ref.shape[1]

    @pl.when(pl.program_id(0) == 0)
    def _():
        high_ref[...], low_ref[...] = split(coeffs_ref[...])

    raw = raw_ref[...].reshape(-1, raw_ref.shape[2])
    done = product(split(raw), (high_ref[...], low_ref[...]))
    out_ref[:, :depth] = done.reshape(raw_ref.shape[0], depth, -1)
    out_ref[:, depth:] = jnp.full((out_ref.shape[0], 8, out_ref.shape[2]), eps_ref[0], jnp.float32)


def fit_kernel(
    got_ref, metric_ref, there_ref, mate_ref, out_ref, eps_ref,
    rows_high, rows_low, square_high, square_low,
):
    rep = lax.axis_index("rep")
    core = lax.axis_index("blk") % 2
    depth = got_ref.shape[1] - 8
    wide = metric_ref.shape[1]
    half, step = wide // 2, wide // 4
    rows = split(got_ref[:, :depth].reshape(-1, got_ref.shape[2]).T)
    for part in range(2):
        at = slice(part * wide, (part + 1) * wide)
        rows_high[part], rows_low[part] = rows[0][:, at], rows[1][:, at]
    out_ref[rep] = product(rows, split(metric_ref[...]))
    for ref, which in ((there_ref, core), (mate_ref, 1 - core)):
        for row, column, piece in (
            (which * half, which * half, ref[:half]),
            (which * step, half, ref[half:]),
            (half, which * step, ref[half:].T),
        ):
            at = pl.ds(pl.multiple_of(row, step), piece.shape[0])
            to = pl.ds(pl.multiple_of(column, step), piece.shape[1])
            square_high[at, to], square_low[at, to] = split(piece)
    mine = metric_ref[pl.ds(pl.multiple_of((1 - rep) * wide, wide), wide)]
    out_ref[1 - rep] = product((rows_high[rep], rows_low[rep]), split(mine), 1, 1) + product(
        (rows_high[1 - rep], rows_low[1 - rep]), (square_high[...], square_low[...])
    )
    eps_ref[...] = got_ref[:, depth:]


def coulomb(own, other_ref):
    total = 0.0
    for half in range(2):
        total = total + product(own[half], split(other_ref[half]), 1, 1)
    return total


def amplitude(whole, levels_ref, column_ref, eps_ref, index, other):
    size = eps_ref.shape[2]
    lower = eps_ref[index][:1] + eps_ref[other][:1]
    across = levels_ref[...] - jnp.concatenate([lower] * (whole.shape[1] // size), 1)
    return (2.0 * whole - whole.T) / (column_ref[...] + across)


def gradient(weights, first_ref, second_ref):
    rep = lax.axis_index("rep")
    size = first_ref.shape[1]
    weights = split(weights)
    one = lambda at, ref: product(
        (weights[0][:, at : at + size], weights[1][:, at : at + size]), split(ref[rep])
    )
    return one(0, first_ref) + one(size, second_ref)


def own_parts(high_ref, low_ref):
    return [(high_ref[half], low_ref[half]) for half in range(2)]


def own_kernel(
    fit_ref, over_ref, near_ref, mate_ref, levels_ref, column_ref, eps_ref,
    high_ref, low_ref, near_out, mate_out, total_ref,
):
    size = fit_ref.shape[1]
    for half in range(2):
        high_ref[half, :size], low_ref[half, :size] = split(fit_ref[half])
        high_ref[half, size:], low_ref[half, size:] = split(over_ref[half])
    own = own_parts(high_ref, low_ref)
    whole = 0.0
    for half in range(2):
        whole = whole + product(own[half], own[half], 1, 1)
    block = lax.axis_index("blk")
    weights = amplitude(whole, levels_ref, column_ref, eps_ref, block, block)
    total_ref[...] = gradient(weights, fit_ref, over_ref)
    near_out[...] = coulomb(own, near_ref)
    mate_out[...] = coulomb(own, mate_ref)


def behind(by):
    blocks = lax.axis_size("blk")
    return lax.rem(lax.axis_index("blk") + blocks - by, blocks)


def near_kernel(
    high_ref, low_ref, far_ref, far_over_ref, near_ref, near_over_ref, near_half_ref,
    levels_ref, column_ref, eps_ref, sum_ref, total_ref,
):
    own = own_parts(high_ref, low_ref)
    block = lax.axis_index("blk")
    core = block % 2
    total = sum_ref[...]
    whole = jnp.concatenate([coulomb(own, far_ref), coulomb(own, far_over_ref)], 1)
    weights = amplitude(whole, levels_ref, column_ref, eps_ref, block, jnp.where(core == 0, behind(3), behind(1)))
    total = total + gradient(weights, far_ref, far_over_ref)
    whole = jnp.concatenate([near_half_ref[...], coulomb(own, near_over_ref)], 1)
    weights = amplitude(whole, levels_ref, column_ref, eps_ref, block, behind(2))
    total_ref[...] = total + gradient(weights, near_ref, near_over_ref)


def mate_kernel(
    high_ref, low_ref, mate_ref, mate_over_ref, mate_half_ref,
    levels_ref, column_ref, eps_ref, sum_ref, out_ref,
):
    own = own_parts(high_ref, low_ref)
    rep = lax.axis_index("rep")
    block = lax.axis_index("blk")
    core = block % 2
    size = mate_ref.shape[1]
    whole = jnp.concatenate([mate_half_ref[...], coulomb(own, mate_over_ref)], 1)
    weights = amplitude(whole, levels_ref, column_ref, eps_ref, block, jnp.where(core == 0, behind(1), behind(3)))
    total = sum_ref[...] + gradient(weights, mate_ref, mate_over_ref)
    out_ref[0, pl.ds(pl.multiple_of(rep * size, size), size)] = total[:size]
    out_ref[0, pl.ds(pl.multiple_of((1 - rep) * size, size), size)] = total[size:]


def call(kernel, out, *arrays, flops, scratch=()):
    given = sum(a.size * a.dtype.itemsize for a in arrays)
    made = sum(math.prod(o.shape) * o.dtype.itemsize for o in jax.tree.leaves(out))
    vmem = pl.BlockSpec(memory_space=pltpu.VMEM)
    return pl.pallas_call(
        kernel,
        out_shape=out,
        in_specs=[vmem] * len(arrays),
        out_specs=jax.tree.map(lambda _: vmem, out),
        scratch_shapes=scratch,
        cost_estimate=pl.CostEstimate(flops=flops, bytes_accessed=given + made, transcendentals=0),
        compiler_params=pltpu.CompilerParams(vmem_limit_bytes=VMEM),
    )(*arrays)


def shape(*dims, dtype=jnp.float32):
    return jax.ShapeDtypeStruct(dims, dtype)


def two_replicas(raw_integrals, virtual_coeffs, metric_root, occ_energies, virt_energies):
    blocks = lax.axis_size("blk")
    block = lax.axis_index("blk")
    rep = lax.axis_index("rep")
    core = block % 2
    swap = [(0, 1), (1, 0)]
    mate = [(i, i ^ 1) for i in range(blocks)]
    orbitals, depth, atoms = raw_integrals.shape
    rows = virtual_coeffs.shape[1]
    aux, wide = metric_root.shape
    group = math.gcd(orbitals, 2)
    base, half, step = rep * wide, wide // 2, wide // 4
    quarter = jnp.concatenate(
        [
            lax.dynamic_slice(metric_root, (base + core * half, core * half), (half, half)),
            lax.dynamic_slice(metric_root, (base + core * step, half), (step, half)),
        ]
    )
    there = lax.ppermute(quarter, "rep", swap)
    sent = pl.pallas_call(
        transform_kernel,
        grid=(orbitals // group,),
        in_specs=[
            pl.BlockSpec((group, depth, atoms), lambda i: (i, 0, 0)),
            pl.BlockSpec((atoms, rows), lambda i: (0, 0)),
            pl.BlockSpec(memory_space=pltpu.SMEM),
        ],
        out_specs=pl.BlockSpec((group, depth + 8, rows), lambda i: (i, 0, 0)),
        out_shape=shape(orbitals, depth + 8, rows),
        scratch_shapes=[pltpu.VMEM((atoms, rows), jnp.bfloat16)] * 2,
        cost_estimate=pl.CostEstimate(
            flops=6 * raw_integrals.size * rows,
            bytes_accessed=4 * raw_integrals.size,
            transcendentals=0,
        ),
        name="transform_kernel",
    )(raw_integrals, virtual_coeffs, occ_energies)
    got = lax.all_to_all(sent, "blk", split_axis=0, concat_axis=0, tiled=True)
    there_mate = lax.ppermute(there, "blk", mate)
    fit, eps = call(
        fit_kernel,
        (shape(2, rows, wide), shape(blocks, 8, rows)),
        got, metric_root, there, there_mate,
        flops=6 * aux * aux * rows,
        scratch=[pltpu.VMEM((2, rows, wide), jnp.bfloat16)] * 2
        + [pltpu.VMEM((wide, wide), jnp.bfloat16)] * 2,
    )
    over = lax.ppermute(fit, "rep", swap)
    near = from_behind(fit, "blk", 2)
    fit_late, over = lax.optimization_barrier((fit, over))
    past = [(i, (i + 1 + 2 * (i % 2)) % blocks) for i in range(blocks)]
    far_over = lax.ppermute(over, "blk", past)
    far = lax.ppermute(fit_late, "blk", past)
    near_over = lax.ppermute(near, "rep", swap)
    near_mate = lax.ppermute(near, "blk", mate)
    levels = jnp.where(rep == 0, virt_energies, jnp.roll(virt_energies, rows))
    levels = (levels[None, :], levels[:, None])
    both = 2 * rows
    halves = shape(2, both, wide, dtype=jnp.bfloat16)
    pair = 6 * both * rows * aux
    high, low, near_half, mate_half, total = call(
        own_kernel,
        (halves, halves, shape(both, rows), shape(both, rows), shape(both, wide)),
        fit_late, over, near, near_mate, *levels, eps, flops=5 * pair,
    )
    mate_over = lax.ppermute(near_over, "blk", mate)
    total = call(
        near_kernel, shape(both, wide), high, low, far, far_over, near, near_over,
        near_half, *levels, eps, total, flops=5 * pair,
    )
    return call(
        mate_kernel, shape(1, both, wide), high, low, near_mate, mate_over, mate_half,
        *levels, eps, total, flops=2 * pair,
    )


def per_device(*arrays):
    blocks = lax.axis_size("blk")
    if lax.axis_size("rep") == 2 and TURNS == 2 and blocks % 2 == 0 and arrays[3].shape == (1,):
        return two_replicas(*arrays)
    return any_replicas(*arrays)


def solution(mesh):
    return jax.shard_map(
        per_device,
        mesh=mesh,
        in_specs=(P(None, "blk", None), P(None, "rep"), P(None, "rep"), P("blk"), P()),
        out_specs=P("blk", None, "rep"),
        check_vma=False,
    )
```

```python
import math

import jax
import jax.numpy as jnp
from jax import lax
from jax.experimental import pallas as pl
from jax.experimental.pallas import tpu as pltpu
from jax.sharding import PartitionSpec as P

TURNS = 2
VMEM = 24 << 20


def from_behind(x, axis, by):
    count = lax.axis_size(axis)
    return lax.ppermute(x, axis, [(i, (i + by) % count) for i in range(count)])


def pair_terms(own_rows, own_eps, other_rows, other_eps, virt_energies, gradient):
    highest = lax.Precision.HIGHEST
    coulomb = jnp.einsum("xaq,ybq->xyab", own_rows, other_rows, precision=highest)
    spread = virt_energies[:, None] + virt_energies[None, :]
    denominator = spread[None, None] - own_eps[:, None, None, None] - other_eps[None, :, None, None]
    amplitude = (2.0 * coulomb - jnp.swapaxes(coulomb, 2, 3)) / denominator
    return gradient + jnp.einsum("xyab,ybq->xaq", amplitude, other_rows, precision=highest)


def any_replicas(raw_integrals, virtual_coeffs, metric_root, occ_energies, virt_energies):
    highest = lax.Precision.HIGHEST
    halfway = jnp.einsum("ipm,ma->ipa", raw_integrals, virtual_coeffs, precision=highest)
    regrouped = lax.all_to_all(halfway, "blk", split_axis=0, concat_axis=1, tiled=True)
    complete = lax.all_gather(regrouped, "rep", axis=2, tiled=True)
    fitted_part = jnp.einsum("xpa,pq->xaq", complete, metric_root, precision=highest)
    fitted = lax.all_gather(fitted_part, "rep", axis=2, tiled=True)
    replica = lax.axis_index("rep")
    replicas = lax.axis_size("rep")
    travel_rows = fitted
    travel_eps = occ_energies
    for bit_index in range((replicas - 1).bit_length()):
        shifted_rows, shifted_eps = from_behind(
            (travel_rows, travel_eps), "blk", (1 << bit_index) * TURNS
        )
        chosen = replica >> bit_index & 1 == 1
        travel_rows = jnp.where(chosen, shifted_rows, travel_rows)
        travel_eps = jnp.where(chosen, shifted_eps, travel_eps)
    gradient = jnp.zeros(fitted.shape, jnp.float32)

    def advance(turn_index, state_now):
        other_rows, other_eps, total = state_now
        total = pair_terms(fitted, occ_energies, other_rows, other_eps, virt_energies, total)
        other_rows, other_eps = from_behind((other_rows, other_eps), "blk", 1)
        return (other_rows, other_eps, total)

    travel_rows, travel_eps, gradient = lax.fori_loop(
        0, TURNS - 1, advance, (travel_rows, travel_eps, gradient)
    )
    gradient = pair_terms(fitted, occ_energies, travel_rows, travel_eps, virt_energies, gradient)
    return lax.psum_scatter(gradient, "rep", scatter_dimension=2, tiled=True)


def split(x):
    high = x.astype(jnp.bfloat16)
    return high, (x - high.astype(jnp.float32)).astype(jnp.bfloat16)


def product(x, y, over_x=1, over_y=0):
    one = lambda p, q: lax.dot_general(
        p, q, (((over_x,), (over_y,)), ((), ())), preferred_element_type=jnp.float32
    )
    return one(x[0], y[0]) + (one(x[0], y[1]) + one(x[1], y[0]))


def transform_kernel(
    raw_hbm, coeffs_hbm, eps_ref, out_hbm, raw_ref, coeffs_ref, out_ref, coeffs_sem, in_sems, out_sems
):
    steps = in_sems.shape[0]
    group = raw_ref.shape[0] // steps
    depth, rows = raw_ref.shape[1], coeffs_ref.shape[1]
    parts = [pl.ds(step * group, group) for step in range(steps)]
    first = pltpu.make_async_copy(coeffs_hbm, coeffs_ref, coeffs_sem)
    first.start()
    into = [
        pltpu.make_async_copy(raw_hbm.at[at], raw_ref.at[at], in_sems.at[step])
        for step, at in enumerate(parts)
    ]
    out = [
        pltpu.make_async_copy(out_ref.at[at], out_hbm.at[at], out_sems.at[step])
        for step, at in enumerate(parts)
    ]
    for copy in into:
        copy.start()
    out_ref[:, depth:] = jnp.full((out_ref.shape[0], 8, rows), eps_ref[0], jnp.float32)
    first.wait()
    high, low = split(coeffs_ref[...])
    both = jnp.concatenate([high, low], 1)
    one = lambda x, y: lax.dot_general(
        x, y, (((1,), (0,)), ((), ())), preferred_element_type=jnp.float32
    )
    for step, at in enumerate(parts):
        into[step].wait()
        raw = split(raw_ref[at].reshape(group * depth, -1))
        wide = one(raw[0], both)
        done = wide[:, :rows] + (wide[:, rows:] + one(raw[1], high))
        out_ref[at, :depth] = done.reshape(group, depth, rows)
        out[step].start()
    for copy in out:
        copy.wait()


def fit_kernel(
    got_ref, metric_ref, there_ref, mate_ref, out_ref, first_ref, second_ref, eps_ref,
    rows_high, rows_low, square_high, square_low,
):
    rep = lax.axis_index("rep")
    core = lax.axis_index("blk") % 2
    depth = got_ref.shape[1] - 8
    wide = metric_ref.shape[1]
    half, step = wide // 2, wide // 4
    rows = split(got_ref[:, :depth].reshape(-1, got_ref.shape[2]).T)
    for part in range(2):
        at = slice(part * wide, (part + 1) * wide)
        rows_high[part], rows_low[part] = rows[0][:, at], rows[1][:, at]
    mine = product(rows, split(metric_ref[...]))
    for ref, which in ((there_ref, core), (mate_ref, 1 - core)):
        for row, column, piece in (
            (which * half, which * half, ref[:half]),
            (which * step, half, ref[half:]),
            (half, which * step, ref[half:].T),
        ):
            at = pl.ds(pl.multiple_of(row, step), piece.shape[0])
            to = pl.ds(pl.multiple_of(column, step), piece.shape[1])
            square_high[at, to], square_low[at, to] = split(piece)
    from_rows = metric_ref[pl.ds(pl.multiple_of((1 - rep) * wide, wide), wide)]
    there = product((rows_high[rep], rows_low[rep]), split(from_rows), 1, 1) + product(
        (rows_high[1 - rep], rows_low[1 - rep]), (square_high[...], square_low[...])
    )
    first_ref[...] = jnp.where(rep == 0, mine, there)
    second_ref[...] = jnp.where(rep == 0, there, mine)
    out_ref[rep] = mine
    out_ref[1 - rep] = there
    eps_ref[...] = got_ref[:, depth:]


def beside(own, others):
    other = split(jnp.concatenate(others, 0))
    count = other[0].shape[0]
    if count == own[0].shape[0]:
        return product(own, other, 1, 1)
    one = lambda x, y: lax.dot_general(
        x, y, (((1,), (1,)), ((), ())), preferred_element_type=jnp.float32
    )
    wide = one(own[0], jnp.concatenate(other, 0))
    return wide[:, :count] + (wide[:, count:] + one(own[1], other[0]))


def amplitude(whole, levels_ref, column_ref, eps_ref, index, other):
    size = eps_ref.shape[2]
    lower = eps_ref[index][:1] + eps_ref[other][:1]
    across = levels_ref[...] - jnp.concatenate([lower] * (whole.shape[1] // size), 1)
    return (2.0 * whole - whole.T) / (column_ref[...] + across)


def gradient(weights, first, second):
    return product(split(weights), split(jnp.concatenate([first, second], 0)))


def half_here(first_ref, second_ref):
    return jnp.where(lax.axis_index("rep") == 0, first_ref[...], second_ref[...])


def own_parts(high_ref, low_ref):
    return [(high_ref[half], low_ref[half]) for half in range(2)]


def own_kernel(
    fit_ref, over_ref, near0_ref, near1_ref, mate0_ref, mate1_ref, levels_ref, column_ref, eps_ref,
    high_ref, low_ref, halves_ref, total_ref,
):
    size = fit_ref.shape[1]
    rep = lax.axis_index("rep")
    for half in range(2):
        high_ref[half, :size], low_ref[half, :size] = split(fit_ref[half])
        high_ref[half, size:], low_ref[half, size:] = split(over_ref[half])
    own = own_parts(high_ref, low_ref)
    whole = product(own[0], own[0], 1, 1) + product(own[1], own[1], 1, 1)
    block = lax.axis_index("blk")
    weights = amplitude(whole, levels_ref, column_ref, eps_ref, block, block)
    total_ref[...] = gradient(weights, fit_ref[rep], over_ref[rep])
    halves_ref[...] = beside(own[0], [near0_ref[...], mate0_ref[...]]) + beside(
        own[1], [near1_ref[...], mate1_ref[...]]
    )


def over_kernel(high_ref, low_ref, near_over_ref, mate_over_ref, halves_ref):
    own = (high_ref[0], low_ref[0])
    halves_ref[...] = beside(own, [near_over_ref[...], mate_over_ref[...]])


def behind(by):
    blocks = lax.axis_size("blk")
    return lax.rem(lax.axis_index("blk") + blocks - by, blocks)


def near_kernel(
    high_ref, low_ref, near0_ref, near1_ref, over0_ref, over1_ref, halves_ref, over_halves_ref,
    levels_ref, column_ref, eps_ref, sum_ref, total_ref,
):
    size = near0_ref.shape[0]
    late = over_halves_ref[:, :size] + beside((high_ref[1], low_ref[1]), [over1_ref[...]])
    whole = jnp.concatenate([halves_ref[:, :size], late], 1)
    block = lax.axis_index("blk")
    weights = amplitude(whole, levels_ref, column_ref, eps_ref, block, behind(2))
    total_ref[...] = sum_ref[...] + gradient(
        weights, half_here(near0_ref, near1_ref), half_here(over0_ref, over1_ref)
    )


def mate_kernel(
    high_ref, low_ref, mate0_ref, mate1_ref, over0_ref, over1_ref, halves_ref, over_halves_ref,
    levels_ref, column_ref, eps_ref, sum_ref, total_ref,
):
    size = mate0_ref.shape[0]
    late = over_halves_ref[:, size:] + beside((high_ref[1], low_ref[1]), [over1_ref[...]])
    whole = jnp.concatenate([halves_ref[:, size:], late], 1)
    block = lax.axis_index("blk")
    other = jnp.where(block % 2 == 0, behind(1), behind(3))
    weights = amplitude(whole, levels_ref, column_ref, eps_ref, block, other)
    total_ref[...] = sum_ref[...] + gradient(
        weights, half_here(mate0_ref, mate1_ref), half_here(over0_ref, over1_ref)
    )


def far_kernel(
    high_ref, low_ref, far_ref, far_over_ref, levels_ref, column_ref, eps_ref, sum_ref, out_ref,
):
    own = own_parts(high_ref, low_ref)
    rep = lax.axis_index("rep")
    size = far_ref.shape[1]
    whole = beside(own[0], [far_ref[0], far_over_ref[0]]) + beside(
        own[1], [far_ref[1], far_over_ref[1]]
    )
    block = lax.axis_index("blk")
    other = jnp.where(block % 2 == 0, behind(3), behind(1))
    weights = amplitude(whole, levels_ref, column_ref, eps_ref, block, other)
    total = sum_ref[...] + gradient(weights, far_ref[rep], far_over_ref[rep])
    out_ref[0, pl.ds(pl.multiple_of(rep * size, size), size)] = total[:size]
    out_ref[0, pl.ds(pl.multiple_of((1 - rep) * size, size), size)] = total[size:]


def call(kernel, out, *arrays, flops, scratch=()):
    given = sum(a.size * a.dtype.itemsize for a in arrays)
    made = sum(math.prod(o.shape) * o.dtype.itemsize for o in jax.tree.leaves(out))
    vmem = pl.BlockSpec(memory_space=pltpu.VMEM)
    return pl.pallas_call(
        kernel,
        out_shape=out,
        in_specs=[vmem] * len(arrays),
        out_specs=jax.tree.map(lambda _: vmem, out),
        scratch_shapes=scratch,
        cost_estimate=pl.CostEstimate(flops=flops, bytes_accessed=given + made, transcendentals=0),
        compiler_params=pltpu.CompilerParams(vmem_limit_bytes=VMEM),
    )(*arrays)


def shape(*dims, dtype=jnp.float32):
    return jax.ShapeDtypeStruct(dims, dtype)


def two_replicas(raw_integrals, virtual_coeffs, metric_root, occ_energies, virt_energies):
    blocks = lax.axis_size("blk")
    block = lax.axis_index("blk")
    rep = lax.axis_index("rep")
    core = block % 2
    swap = [(0, 1), (1, 0)]
    mate = [(i, i ^ 1) for i in range(blocks)]
    orbitals, depth, _ = raw_integrals.shape
    rows = virtual_coeffs.shape[1]
    aux, wide = metric_root.shape
    steps = math.gcd(orbitals, 8)
    anywhere = pl.BlockSpec(memory_space=pl.ANY)
    sent = pl.pallas_call(
        transform_kernel,
        in_specs=[anywhere, anywhere, pl.BlockSpec(memory_space=pltpu.SMEM)],
        out_specs=anywhere,
        out_shape=shape(orbitals, depth + 8, rows),
        scratch_shapes=[
            pltpu.VMEM(raw_integrals.shape, jnp.float32),
            pltpu.VMEM(virtual_coeffs.shape, jnp.float32),
            pltpu.VMEM((orbitals, depth + 8, rows), jnp.float32),
            pltpu.SemaphoreType.DMA,
            pltpu.SemaphoreType.DMA((steps,)),
            pltpu.SemaphoreType.DMA((steps,)),
        ],
        cost_estimate=pl.CostEstimate(
            flops=6 * raw_integrals.size * rows,
            bytes_accessed=4 * raw_integrals.size,
            transcendentals=0,
        ),
        name="transform_kernel",
    )(raw_integrals, virtual_coeffs, occ_energies)
    base, half, step = rep * wide, wide // 2, wide // 4
    quarter = jnp.concatenate(
        [
            lax.dynamic_slice(metric_root, (base + core * half, core * half), (half, half)),
            lax.dynamic_slice(metric_root, (base + core * step, half), (step, half)),
        ]
    )
    there = lax.ppermute(quarter, "rep", swap)
    got = lax.all_to_all(sent, "blk", split_axis=0, concat_axis=0, tiled=True)
    there_mate = lax.ppermute(there, "blk", mate)
    piece = shape(rows, wide)
    fit, first, second, eps = call(
        fit_kernel,
        (shape(2, rows, wide), piece, piece, shape(blocks, 8, rows)),
        got, metric_root, there, there_mate,
        flops=6 * aux * aux * rows,
        scratch=[pltpu.VMEM((2, rows, wide), jnp.bfloat16)] * 2
        + [pltpu.VMEM((wide, wide), jnp.bfloat16)] * 2,
    )
    past = [(i, (i + 1 + 2 * (i % 2)) % blocks) for i in range(blocks)]
    near0 = from_behind(first, "blk", 2)
    over = lax.ppermute(fit, "rep", swap)
    near1 = from_behind(second, "blk", 2)
    near_over0 = lax.ppermute(near0, "rep", swap)
    far = lax.ppermute(fit, "blk", past)
    far_over = lax.ppermute(over, "blk", past)
    near_over1 = lax.ppermute(near1, "rep", swap)
    mate0 = lax.ppermute(near0, "blk", mate)
    mate1 = lax.ppermute(near1, "blk", mate)
    levels = jnp.where(rep == 0, virt_energies, jnp.roll(virt_energies, rows))
    levels = (levels[None, :], levels[:, None])
    both = 2 * rows
    parts = shape(2, both, wide, dtype=jnp.bfloat16)
    pair = 6 * both * rows * aux
    high, low, halves, total = call(
        own_kernel,
        (parts, parts, shape(both, both), shape(both, wide)),
        fit, over, near0, near1, mate0, mate1, *levels, eps, flops=5 * pair,
    )
    mate_over0 = lax.ppermute(near_over0, "blk", mate)
    over_halves = call(
        over_kernel, shape(both, both), high, low, near_over0, mate_over0, flops=pair
    )
    mate_over1 = lax.ppermute(near_over1, "blk", mate)
    total = call(
        near_kernel, shape(both, wide), high, low, near0, near1, near_over0, near_over1,
        halves, over_halves, *levels, eps, total, flops=2 * pair,
    )
    total = call(
        mate_kernel, shape(both, wide), high, low, mate0, mate1, mate_over0, mate_over1,
        halves, over_halves, *levels, eps, total, flops=2 * pair,
    )
    return call(
        far_kernel, shape(1, both, wide), high, low, far, far_over, *levels, eps, total,
        flops=3 * pair,
    )


def per_device(*arrays):
    blocks = lax.axis_size("blk")
    if lax.axis_size("rep") == 2 and TURNS == 2 and blocks % 2 == 0 and arrays[3].shape == (1,):
        return two_replicas(*arrays)
    return any_replicas(*arrays)


def solution(mesh):
    return jax.shard_map(
        per_device,
        mesh=mesh,
        in_specs=(P(None, "blk", None), P(None, "rep"), P(None, "rep"), P("blk"), P()),
        out_specs=P("blk", None, "rep"),
        check_vma=False,
    )
```

```python
import math

import jax
import jax.numpy as jnp
from jax import lax
from jax.experimental import pallas as pl
from jax.experimental.pallas import tpu as pltpu
from jax.sharding import PartitionSpec as P

TURNS = 2
OWN, NEAR, FAR, MATE = range(4)
VMEM = 24 << 20


def from_behind(x, axis, by):
    count = lax.axis_size(axis)
    return lax.ppermute(x, axis, [(i, (i + by) % count) for i in range(count)])


def pair_terms(own_rows, own_eps, other_rows, other_eps, virt_energies, gradient):
    highest = lax.Precision.HIGHEST
    coulomb = jnp.einsum("xaq,ybq->xyab", own_rows, other_rows, precision=highest)
    spread = virt_energies[:, None] + virt_energies[None, :]
    denominator = spread[None, None] - own_eps[:, None, None, None] - other_eps[None, :, None, None]
    amplitude = (2.0 * coulomb - jnp.swapaxes(coulomb, 2, 3)) / denominator
    return gradient + jnp.einsum("xyab,ybq->xaq", amplitude, other_rows, precision=highest)


def any_replicas(raw_integrals, virtual_coeffs, metric_root, occ_energies, virt_energies):
    highest = lax.Precision.HIGHEST
    halfway = jnp.einsum("ipm,ma->ipa", raw_integrals, virtual_coeffs, precision=highest)
    regrouped = lax.all_to_all(halfway, "blk", split_axis=0, concat_axis=1, tiled=True)
    complete = lax.all_gather(regrouped, "rep", axis=2, tiled=True)
    fitted_part = jnp.einsum("xpa,pq->xaq", complete, metric_root, precision=highest)
    fitted = lax.all_gather(fitted_part, "rep", axis=2, tiled=True)
    replica = lax.axis_index("rep")
    replicas = lax.axis_size("rep")
    travel_rows = fitted
    travel_eps = occ_energies
    for bit_index in range((replicas - 1).bit_length()):
        shifted_rows, shifted_eps = from_behind(
            (travel_rows, travel_eps), "blk", (1 << bit_index) * TURNS
        )
        chosen = replica >> bit_index & 1 == 1
        travel_rows = jnp.where(chosen, shifted_rows, travel_rows)
        travel_eps = jnp.where(chosen, shifted_eps, travel_eps)
    gradient = jnp.zeros(fitted.shape, jnp.float32)

    def advance(turn_index, state_now):
        other_rows, other_eps, total = state_now
        total = pair_terms(fitted, occ_energies, other_rows, other_eps, virt_energies, total)
        other_rows, other_eps = from_behind((other_rows, other_eps), "blk", 1)
        return (other_rows, other_eps, total)

    travel_rows, travel_eps, gradient = lax.fori_loop(
        0, TURNS - 1, advance, (travel_rows, travel_eps, gradient)
    )
    gradient = pair_terms(fitted, occ_energies, travel_rows, travel_eps, virt_energies, gradient)
    return lax.psum_scatter(gradient, "rep", scatter_dimension=2, tiled=True)


def split(x):
    high = x.astype(jnp.bfloat16)
    return high, (x - high.astype(jnp.float32)).astype(jnp.bfloat16)


def product(x, y, over_x=1, over_y=0):
    one = lambda p, q: lax.dot_general(
        p, q, (((over_x,), (over_y,)), ((), ())), preferred_element_type=jnp.float32
    )
    return one(x[0], y[0]) + (one(x[0], y[1]) + one(x[1], y[0]))


def transform_kernel(
    raw_hbm, coeffs_hbm, out_hbm, raw_ref, coeffs_ref, out_ref, coeffs_sem, in_sems, out_sems
):
    steps = in_sems.shape[0]
    group = raw_ref.shape[0] // steps
    depth, rows = raw_ref.shape[1], coeffs_ref.shape[1]
    parts = [pl.ds(step * group, group) for step in range(steps)]
    first = pltpu.make_async_copy(coeffs_hbm, coeffs_ref, coeffs_sem)
    first.start()
    into = [
        pltpu.make_async_copy(raw_hbm.at[at], raw_ref.at[at], in_sems.at[step])
        for step, at in enumerate(parts)
    ]
    out = [
        pltpu.make_async_copy(out_ref.at[at], out_hbm.at[at], out_sems.at[step])
        for step, at in enumerate(parts)
    ]
    for copy in into:
        copy.start()
    first.wait()
    high, low = split(coeffs_ref[...])
    both = jnp.concatenate([high, low], 1)
    one = lambda x, y: lax.dot_general(
        x, y, (((1,), (0,)), ((), ())), preferred_element_type=jnp.float32
    )
    for step, at in enumerate(parts):
        into[step].wait()
        raw = split(raw_ref[at].reshape(group * depth, -1))
        wide = one(raw[0], both)
        done = wide[:, :rows] + (wide[:, rows:] + one(raw[1], high))
        out_ref[at] = done.reshape(group, depth, rows)
        out[step].start()
    for copy in out:
        copy.wait()


def levels_kernel(own_eps, near_eps, far_eps, mate_eps, eps_ref):
    for index, level in enumerate((own_eps, near_eps, far_eps, mate_eps)):
        eps_ref[index] = jnp.broadcast_to(level[...], eps_ref.shape[1:])


def fit_kernel(
    got_ref, metric_ref, there_ref, mate_ref, out_ref, first_ref, second_ref,
    rows_high, rows_low, square_high, square_low,
):
    rep = lax.axis_index("rep")
    core = lax.axis_index("blk") % 2
    wide = metric_ref.shape[1]
    half, step = wide // 2, wide // 4
    rows = split(got_ref[...].reshape(-1, got_ref.shape[2]).T)
    for part in range(2):
        at = slice(part * wide, (part + 1) * wide)
        rows_high[part], rows_low[part] = rows[0][:, at], rows[1][:, at]
    mine = product(rows, split(metric_ref[...]))
    for ref, which in ((there_ref, core), (mate_ref, 1 - core)):
        for row, column, piece in (
            (which * half, which * half, ref[:half]),
            (which * step, half, ref[half:]),
            (half, which * step, ref[half:].T),
        ):
            at = pl.ds(pl.multiple_of(row, step), piece.shape[0])
            to = pl.ds(pl.multiple_of(column, step), piece.shape[1])
            square_high[at, to], square_low[at, to] = split(piece)
    from_rows = metric_ref[pl.ds(pl.multiple_of((1 - rep) * wide, wide), wide)]
    there = product((rows_high[rep], rows_low[rep]), split(from_rows), 1, 1) + product(
        (rows_high[1 - rep], rows_low[1 - rep]), (square_high[...], square_low[...])
    )
    first_ref[...] = jnp.where(rep == 0, mine, there)
    second_ref[...] = jnp.where(rep == 0, there, mine)
    out_ref[rep] = mine
    out_ref[1 - rep] = there


def beside(own, others):
    other = split(jnp.concatenate(others, 0))
    count = other[0].shape[0]
    if count == own[0].shape[0]:
        return product(own, other, 1, 1)
    one = lambda x, y: lax.dot_general(
        x, y, (((1,), (1,)), ((), ())), preferred_element_type=jnp.float32
    )
    wide = one(own[0], jnp.concatenate(other, 0))
    return wide[:, :count] + (wide[:, count:] + one(own[1], other[0]))


def amplitude(whole, levels_ref, column_ref, eps_ref, index, other):
    size = eps_ref.shape[2]
    lower = eps_ref[index][:1] + eps_ref[other][:1]
    across = levels_ref[...] - jnp.concatenate([lower] * (whole.shape[1] // size), 1)
    return (2.0 * whole - whole.T) / (column_ref[...] + across)


def gradient(weights, first, second):
    return product(split(weights), split(jnp.concatenate([first, second], 0)))


def half_here(first_ref, second_ref):
    return jnp.where(lax.axis_index("rep") == 0, first_ref[...], second_ref[...])


def own_parts(high_ref, low_ref):
    return [(high_ref[half], low_ref[half]) for half in range(2)]


def own_kernel(
    fit_ref, over_ref, near0_ref, near1_ref, mate0_ref, mate1_ref, levels_ref, column_ref, eps_ref,
    high_ref, low_ref, halves_ref, total_ref,
):
    size = fit_ref.shape[1]
    rep = lax.axis_index("rep")
    for half in range(2):
        high_ref[half, :size], low_ref[half, :size] = split(fit_ref[half])
        high_ref[half, size:], low_ref[half, size:] = split(over_ref[half])
    own = own_parts(high_ref, low_ref)
    whole = product(own[0], own[0], 1, 1) + product(own[1], own[1], 1, 1)
    weights = amplitude(whole, levels_ref, column_ref, eps_ref, OWN, OWN)
    total_ref[...] = gradient(weights, fit_ref[rep], over_ref[rep])
    halves_ref[...] = beside(own[0], [near0_ref[...], mate0_ref[...]]) + beside(
        own[1], [near1_ref[...], mate1_ref[...]]
    )


def over_kernel(high_ref, low_ref, near_over_ref, mate_over_ref, halves_ref):
    own = (high_ref[0], low_ref[0])
    halves_ref[...] = beside(own, [near_over_ref[...], mate_over_ref[...]])


def near_kernel(
    high_ref, low_ref, near0_ref, near1_ref, over0_ref, over1_ref, halves_ref, over_halves_ref,
    levels_ref, column_ref, eps_ref, sum_ref, total_ref,
):
    size = near0_ref.shape[0]
    late = over_halves_ref[:, :size] + beside((high_ref[1], low_ref[1]), [over1_ref[...]])
    whole = jnp.concatenate([halves_ref[:, :size], late], 1)
    weights = amplitude(whole, levels_ref, column_ref, eps_ref, OWN, NEAR)
    total_ref[...] = sum_ref[...] + gradient(
        weights, half_here(near0_ref, near1_ref), half_here(over0_ref, over1_ref)
    )


def mate_kernel(
    high_ref, low_ref, mate0_ref, mate1_ref, over0_ref, over1_ref, halves_ref, over_halves_ref,
    levels_ref, column_ref, eps_ref, sum_ref, total_ref,
):
    size = mate0_ref.shape[0]
    late = over_halves_ref[:, size:] + beside((high_ref[1], low_ref[1]), [over1_ref[...]])
    whole = jnp.concatenate([halves_ref[:, size:], late], 1)
    weights = amplitude(whole, levels_ref, column_ref, eps_ref, OWN, MATE)
    total_ref[...] = sum_ref[...] + gradient(
        weights, half_here(mate0_ref, mate1_ref), half_here(over0_ref, over1_ref)
    )


def far_kernel(
    high_ref, low_ref, far_ref, far_over_ref, levels_ref, column_ref, eps_ref, sum_ref, out_ref,
):
    own = own_parts(high_ref, low_ref)
    rep = lax.axis_index("rep")
    size = far_ref.shape[1]
    whole = beside(own[0], [far_ref[0], far_over_ref[0]]) + beside(
        own[1], [far_ref[1], far_over_ref[1]]
    )
    weights = amplitude(whole, levels_ref, column_ref, eps_ref, OWN, FAR)
    total = sum_ref[...] + gradient(weights, far_ref[rep], far_over_ref[rep])
    out_ref[0, pl.ds(pl.multiple_of(rep * size, size), size)] = total[:size]
    out_ref[0, pl.ds(pl.multiple_of((1 - rep) * size, size), size)] = total[size:]


def call(kernel, out, *arrays, flops, scratch=()):
    given = sum(a.size * a.dtype.itemsize for a in arrays)
    made = sum(math.prod(o.shape) * o.dtype.itemsize for o in jax.tree.leaves(out))
    vmem = pl.BlockSpec(memory_space=pltpu.VMEM)
    return pl.pallas_call(
        kernel,
        out_shape=out,
        in_specs=[vmem] * len(arrays),
        out_specs=jax.tree.map(lambda _: vmem, out),
        scratch_shapes=scratch,
        cost_estimate=pl.CostEstimate(flops=flops, bytes_accessed=given + made, transcendentals=0),
        compiler_params=pltpu.CompilerParams(vmem_limit_bytes=VMEM),
    )(*arrays)


def shape(*dims, dtype=jnp.float32):
    return jax.ShapeDtypeStruct(dims, dtype)


def two_replicas(raw_integrals, virtual_coeffs, metric_root, occ_energies, virt_energies):
    blocks = lax.axis_size("blk")
    block = lax.axis_index("blk")
    rep = lax.axis_index("rep")
    core = block % 2
    swap = [(0, 1), (1, 0)]
    mate = [(i, i ^ 1) for i in range(blocks)]
    orbitals, depth, _ = raw_integrals.shape
    rows = virtual_coeffs.shape[1]
    aux, wide = metric_root.shape
    steps = math.gcd(orbitals, 8)
    anywhere = pl.BlockSpec(memory_space=pl.ANY)
    sent = pl.pallas_call(
        transform_kernel,
        in_specs=[anywhere, anywhere],
        out_specs=anywhere,
        out_shape=shape(orbitals, depth, rows),
        scratch_shapes=[
            pltpu.VMEM(raw_integrals.shape, jnp.float32),
            pltpu.VMEM(virtual_coeffs.shape, jnp.float32),
            pltpu.VMEM((orbitals, depth, rows), jnp.float32),
            pltpu.SemaphoreType.DMA,
            pltpu.SemaphoreType.DMA((steps,)),
            pltpu.SemaphoreType.DMA((steps,)),
        ],
        cost_estimate=pl.CostEstimate(
            flops=6 * raw_integrals.size * rows,
            bytes_accessed=4 * raw_integrals.size,
            transcendentals=0,
        ),
        name="transform_kernel",
    )(raw_integrals, virtual_coeffs)
    base, half, step = rep * wide, wide // 2, wide // 4
    quarter = jnp.concatenate(
        [
            lax.dynamic_slice(metric_root, (base + core * half, core * half), (half, half)),
            lax.dynamic_slice(metric_root, (base + core * step, half), (step, half)),
        ]
    )
    there = lax.ppermute(quarter, "rep", swap)
    got = lax.all_to_all(sent, "blk", split_axis=0, concat_axis=0, tiled=True)
    past = [(i, (i + 1 + 2 * (i % 2)) % blocks) for i in range(blocks)]
    near_eps = from_behind(occ_energies, "blk", 2)
    far_eps = lax.ppermute(occ_energies, "blk", past)
    mate_eps = lax.ppermute(
        occ_energies, "blk", [(i, ((i + 2) % blocks) ^ 1) for i in range(blocks)]
    )
    there_mate = lax.ppermute(there, "blk", mate)
    piece = shape(rows, wide)
    fit, first, second = call(
        fit_kernel,
        (shape(2, rows, wide), piece, piece),
        got, metric_root, there, there_mate,
        flops=6 * aux * aux * rows,
        scratch=[pltpu.VMEM((2, rows, wide), jnp.bfloat16)] * 2
        + [pltpu.VMEM((wide, wide), jnp.bfloat16)] * 2,
    )
    near0 = from_behind(first, "blk", 2)
    over = lax.ppermute(fit, "rep", swap)
    near1 = from_behind(second, "blk", 2)
    near_over0 = lax.ppermute(near0, "rep", swap)
    far = lax.ppermute(fit, "blk", past)
    far_over = lax.ppermute(over, "blk", past)
    near_over1 = lax.ppermute(near1, "rep", swap)
    mate0 = lax.ppermute(near0, "blk", mate)
    mate1 = lax.ppermute(near1, "blk", mate)
    eps = call(
        levels_kernel, shape(4, 8, rows),
        *(a.reshape(1, 1) for a in (occ_energies, near_eps, far_eps, mate_eps)), flops=0,
    )
    levels = jnp.where(rep == 0, virt_energies, jnp.roll(virt_energies, rows))
    levels = (levels[None, :], levels[:, None])
    both = 2 * rows
    parts = shape(2, both, wide, dtype=jnp.bfloat16)
    pair = 6 * both * rows * aux
    high, low, halves, total = call(
        own_kernel,
        (parts, parts, shape(both, both), shape(both, wide)),
        fit, over, near0, near1, mate0, mate1, *levels, eps, flops=5 * pair,
    )
    mate_over0 = lax.ppermute(near_over0, "blk", mate)
    over_halves = call(
        over_kernel, shape(both, both), high, low, near_over0, mate_over0, flops=pair
    )
    mate_over1 = lax.ppermute(near_over1, "blk", mate)
    total = call(
        near_kernel, shape(both, wide), high, low, near0, near1, near_over0, near_over1,
        halves, over_halves, *levels, eps, total, flops=2 * pair,
    )
    total = call(
        mate_kernel, shape(both, wide), high, low, mate0, mate1, mate_over0, mate_over1,
        halves, over_halves, *levels, eps, total, flops=2 * pair,
    )
    return call(
        far_kernel, shape(1, both, wide), high, low, far, far_over, *levels, eps, total,
        flops=3 * pair,
    )


def per_device(*arrays):
    blocks = lax.axis_size("blk")
    if lax.axis_size("rep") == 2 and TURNS == 2 and blocks % 2 == 0 and arrays[3].shape == (1,):
        return two_replicas(*arrays)
    return any_replicas(*arrays)


def solution(mesh):
    return jax.shard_map(
        per_device,
        mesh=mesh,
        in_specs=(P(None, "blk", None), P(None, "rep"), P(None, "rep"), P("blk"), P()),
        out_specs=P("blk", None, "rep"),
        check_vma=False,
    )
```
